32 devices in a mesh: groups: 2 (over y), mp: 4 (over z), dp: 2 (over x), guide: 2 (over core).
Axes of the slice: x: 2, y: 2, z: 4, core: 2. Of those that a mesh axis runs over, the one named last changes fastest.
Arguments:
- tokens: bfloat16 [192, 8192], P(('groups', 'mp'), ('dp', 'guide')), parts along dimension 0, may hold values from -6 to 6
- w_gate: bfloat16 [8192, 14336], P(('dp', 'guide'), 'mp'), may hold values from -0.0625 to 0.0625
- w_up: bfloat16 [8192, 14336], P(('dp', 'guide'), 'mp'), may hold values from -0.0625 to 0.0625
- w_down: bfloat16 [14336, 8192], P('mp', ('dp', 'guide')), may hold values from -0.046875 to 0.046875
Outputs:
- layer_output: bfloat16 [192, 8192], P(('groups', 'mp'), ('dp', 'guide')), parts along dimension 0
The draws below stay inside these ranges and needn't reach their ends.
There are 2 independent parts, one for each index of `groups`. The reference program is written for one: setup_inputs(seed, part) draws one part's arguments, and reference() takes and returns one part's arrays. A program takes and returns all parts, laid end to end along the dimension named above; an argument that names none is the same for every part. Nothing has to cross between parts.
All inputs are finite; a program needn't handle non-finite values.
Results may differ from the reference program's by a relative error of at most 0.0049.
Values may be sent and summed in bfloat16 or wider, within the bound.
A program may use at most 128 MiB of HBM per device.

```python
import jax
import jax.numpy as jnp

D = 8192
FF = 14336
ROWS = 96


def level_of(own_key, shape, split, least, largest):
    level, own = 1.0, jax.random.fold_in(own_key, 6)
    for dim, parts in split:
        steps = jnp.exp(jax.random.uniform(jax.random.fold_in(own, dim), (parts,), jnp.float32, least / len(split), largest / len(split)))
        level = level * jnp.repeat(steps, shape[dim] // parts).reshape([-1 if axis == dim else 1 for axis in range(len(shape))])
    return level


def gaussian(key, dims, deviation, reach, cuts=(), dtype=jnp.bfloat16):
    result = jax.random.normal(key, dims, jnp.float32) * deviation
    if len(cuts) > 0:
        result = level_of(key, dims, cuts, -0.22, 0.18) * result
    return jnp.clip(result, min=-reach, max=reach).astype(dtype)


def setup_inputs(seed: int = 0, part: int = 0) -> dict:
    splits = jax.random.split(jax.random.key(seed), 5)
    part_keys = jax.random.split(jax.random.fold_in(splits[4], part), 5)
    tokens = gaussian(part_keys[0], (ROWS, D), 1.0, 6.0, ((0, 4), (1, 4)))
    w_gate = gaussian(splits[1], (D, FF), D ** -0.5, 0.0625, ((0, 4), (1, 4)))
    w_up = gaussian(splits[2], (D, FF), D ** -0.5, 0.0625, ((0, 4), (1, 4)))
    w_down = gaussian(splits[3], (FF, D), FF ** -0.5, 0.046875, ((0, 4), (1, 4)))
    return dict(tokens=tokens, w_gate=w_gate, w_up=w_up, w_down=w_down)


def reference(tokens, w_gate, w_up, w_down):
    gate_sum = jnp.dot(tokens, w_gate, preferred_element_type=jnp.float32)
    up_sum = jnp.dot(tokens, w_up, preferred_element_type=jnp.float32)
    hidden = (jax.nn.silu(gate_sum) * up_sum).astype(jnp.bfloat16)
    total = jnp.dot(hidden, w_down, preferred_element_type=jnp.float32)
    return total.astype(jnp.bfloat16)
```

```python
import functools

import jax
import jax.numpy as jnp
from jax import lax
from jax.experimental import pallas as pl
from jax.experimental.pallas import tpu as pltpu
from jax.sharding import PartitionSpec as P

MESH = pl.DeviceIdType.MESH
F32, BF16 = jnp.float32, jnp.bfloat16
WIDTH = 256
OUT_WIDTH = 512


def kernel(mp, dp, tokens, w_gate, w_up, w_down, out, *scratch):
    (gate_v, up_v, down_v, tok_in, tok_f, tok, sum1_out, sum1_in, total, kept, sum2_out, sum2_in,
     hid, part, out_kept, out_send, out_recv,
     w_sem, down_sem, tok_own, tok_s, tok_r, s1_s, s1_r, s2_s, s2_r, hx_s, hx_r, hp_s, hp_r, c_s, c_r) = scratch
    m, d, g = lax.axis_index("mp"), lax.axis_index("dp"), lax.axis_index("guide")
    rows = tokens.shape[0]
    n_half = gate_v.shape[0] // 2
    n_out = down_v.shape[0]
    share = rows * mp // dp
    other = 1 - g

    def weights(side, c):
        half = other if side == 0 else g
        cols = pl.ds(pl.multiple_of((half * n_half + c) * WIDTH, WIDTH), WIDTH)
        slot = side * n_half + c
        return (pltpu.make_async_copy(w_gate.at[:, cols], gate_v.at[slot], w_sem.at[0, slot]),
                pltpu.make_async_copy(w_up.at[:, cols], up_v.at[slot], w_sem.at[1, slot]))

    def downs(n):
        return pltpu.make_async_copy(
            w_down.at[:, pl.ds(pl.multiple_of(n * OUT_WIDTH, OUT_WIDTH), OUT_WIDTH)], down_v.at[n], down_sem.at[n])

    own = pltpu.make_async_copy(tokens, tok_in.at[m], tok_own)
    own.start()
    for side in range(2):
        @pl.loop(0, n_half)
        def _(c):
            for copy in weights(side, c):
                copy.start()

    @pl.loop(0, n_out)
    def _(n):
        downs(n).start()

    barrier = pltpu.get_barrier_semaphore()
    for j in range(1, mp):
        pl.semaphore_signal(barrier, inc=1, device_id={"mp": lax.rem(m + j, mp)}, device_id_type=MESH)
    for j in range(1, dp):
        pl.semaphore_signal(barrier, inc=1, device_id={"dp": lax.rem(d + j, dp)}, device_id_type=MESH)
    pl.semaphore_signal(barrier, inc=1, device_id={"guide": other}, device_id_type=MESH)
    pl.semaphore_wait(barrier, mp + dp - 1)

    def tok_copy(j):
        return pltpu.make_async_remote_copy(
            src_ref=tokens, dst_ref=tok_in.at[m], send_sem=tok_s.at[j - 1], recv_sem=tok_r.at[j - 1],
            device_id={"mp": lax.rem(m + j, mp)}, device_id_type=MESH)

    for j in range(mp - 1, 0, -1):
        tok_copy(j).start()
    own.wait()
    for j in range(1, mp):
        tok_copy(j).wait_recv()
    for q in range(mp):
        tok_f[q * rows:(q + 1) * rows, :] = tok_in[q].astype(F32)
    tok[...] = tok_f[...].astype(BF16)

    def s1_copy(c):
        return pltpu.make_async_remote_copy(
            src_ref=sum1_out.at[c], dst_ref=sum1_in.at[c], send_sem=s1_s.at[c], recv_sem=s1_r.at[c],
            device_id={"guide": other}, device_id_type=MESH)

    @pl.loop(0, n_half)
    def _(c):
        for copy in weights(0, c):
            copy.wait()
        sum1_out[c, 0] = jnp.dot(tok[...], gate_v[c], preferred_element_type=F32).astype(BF16)
        sum1_out[c, 1] = jnp.dot(tok[...], up_v[c], preferred_element_type=F32).astype(BF16)
        s1_copy(c).start()

    def s2_copy(c, j):
        return pltpu.make_async_remote_copy(
            src_ref=sum2_out.at[c, j - 1], dst_ref=sum2_in.at[c, j - 1],
            send_sem=s2_s.at[c, j - 1], recv_sem=s2_r.at[c, j - 1],
            device_id={"dp": lax.rem(d + j, dp)}, device_id_type=MESH)

    def rows_of(b):
        return pl.ds(pl.multiple_of(b * share, 16), share)

    @pl.loop(0, n_half)
    def _(c):
        for copy in weights(1, c):
            copy.wait()
        total[0] = jnp.dot(tok[...], gate_v[n_half + c], preferred_element_type=F32)
        total[1] = jnp.dot(tok[...], up_v[n_half + c], preferred_element_type=F32)
        s1_copy(c).wait_recv()
        for j in range(1, dp):
            b = rows_of(lax.rem(d + j, dp))
            for k in range(2):
                sum2_out[c, j - 1, k] = (total[k, b, :] + sum1_in[c, k, b, :].astype(F32)).astype(BF16)
            s2_copy(c, j).start()
        for k in range(2):
            kept[c, k] = total[k, rows_of(d), :] + sum1_in[c, k, rows_of(d), :].astype(F32)

    def block(b, half, c):
        return hid.at[rows_of(b), pl.ds(pl.multiple_of((half * n_half + c) * WIDTH, WIDTH), WIDTH)]

    def hx_copy(c, j):
        return pltpu.make_async_remote_copy(
            src_ref=block(d, g, c), dst_ref=block(d, g, c), send_sem=hx_s.at[c, j - 1], recv_sem=hx_r.at[c, j - 1],
            device_id={"dp": lax.rem(d + j, dp)}, device_id_type=MESH)

    def hp_copy(c, j):
        b = block(lax.rem(d + dp - j, dp), g, c)
        return pltpu.make_async_remote_copy(
            src_ref=b, dst_ref=b, send_sem=hp_s.at[c, j], recv_sem=hp_r.at[c, j],
            device_id={"guide": other}, device_id_type=MESH)

    @pl.loop(0, n_half)
    def _(c):
        for j in range(1, dp):
            s2_copy(c, j).wait_recv()
        gate, up = kept[c, 0], kept[c, 1]
        for j in range(1, dp):
            gate = gate + sum2_in[c, j - 1, 0].astype(F32)
            up = up + sum2_in[c, j - 1, 1].astype(F32)
        block(d, g, c)[...] = (gate / (1.0 + jnp.exp(-gate)) * up).astype(BF16)
        for j in range(1, dp):
            hx_copy(c, j).start()
        hp_copy(c, 0).start()

    @pl.loop(0, n_half)
    def _(c):
        for j in range(1, dp):
            hx_copy(c, j).wait_recv()
            hp_copy(c, j).start()

    @pl.loop(0, n_half)
    def _(c):
        for j in range(dp):
            hp_copy(c, j).wait_recv()

    def c_copy(n, j):
        return pltpu.make_async_remote_copy(
            src_ref=out_send.at[n, j - 1], dst_ref=out_recv.at[n, j - 1],
            send_sem=c_s.at[n, j - 1], recv_sem=c_r.at[n, j - 1],
            device_id={"mp": lax.rem(m + j, mp)}, device_id_type=MESH)

    def out_rows(q):
        return pl.ds(pl.multiple_of(q * rows, 8), rows)

    @pl.loop(0, n_out)
    def _(n):
        downs(n).wait()
        part[...] = jnp.dot(hid[...], down_v[n], preferred_element_type=F32)
        for j in range(mp - 1, 0, -1):
            out_send[n, j - 1] = part[out_rows(lax.rem(m + j, mp)), :].astype(BF16)
            c_copy(n, j).start()
        out_kept[n] = part[out_rows(m), :]

    for n in range(n_out):
        acc = out_kept[n]
        for j in range(1, mp):
            c_copy(n, j).wait_recv()
            acc = acc + out_recv[n, j - 1].astype(F32)
        out[:, n * OUT_WIDTH:(n + 1) * OUT_WIDTH] = acc.astype(BF16)

    for j in range(1, mp):
        tok_copy(j).wait_send()

    @pl.loop(0, n_half)
    def _(c):
        s1_copy(c).wait_send()
        for j in range(1, dp):
            s2_copy(c, j).wait_send()
            hx_copy(c, j).wait_send()
        for j in range(dp):
            hp_copy(c, j).wait_send()

    @pl.loop(0, n_out)
    def _(n):
        for j in range(1, mp):
            c_copy(n, j).wait_send()


def fused(mp, dp, tokens, w_gate, w_up, w_down):
    rows, depth = tokens.shape
    cols, wide = w_gate.shape[1], w_down.shape[1]
    nc, nh, no = cols // WIDTH, cols // WIDTH // 2, wide // OUT_WIDTH
    full, share = rows * mp, rows * mp // dp
    dma = pltpu.SemaphoreType.DMA
    any_, vmem = pl.BlockSpec(memory_space=pl.ANY), pl.BlockSpec(memory_space=pltpu.VMEM)
    return pl.pallas_call(
        functools.partial(kernel, mp, dp),
        out_shape=jax.ShapeDtypeStruct((rows, wide), BF16),
        in_specs=[any_] * 4,
        out_specs=vmem,
        scratch_shapes=[
            pltpu.VMEM((nc, depth, WIDTH), BF16),
            pltpu.VMEM((nc, depth, WIDTH), BF16),
            pltpu.VMEM((no, cols, OUT_WIDTH), BF16),
            pltpu.VMEM((mp, rows, depth), BF16),
            pltpu.VMEM((full, depth), F32),
            pltpu.VMEM((full, depth), BF16),
            pltpu.VMEM((nh, 2, full, WIDTH), BF16),
            pltpu.VMEM((nh, 2, full, WIDTH), BF16),
            pltpu.VMEM((2, full, WIDTH), F32),
            pltpu.VMEM((nh, 2, share, WIDTH), F32),
            pltpu.VMEM((nh, dp - 1, 2, share, WIDTH), BF16),
            pltpu.VMEM((nh, dp - 1, 2, share, WIDTH), BF16),
            pltpu.VMEM((full, cols), BF16),
            pltpu.VMEM((full, OUT_WIDTH), F32),
            pltpu.VMEM((no, rows, OUT_WIDTH), F32),
            pltpu.VMEM((no, mp - 1, rows, OUT_WIDTH), BF16),
            pltpu.VMEM((no, mp - 1, rows, OUT_WIDTH), BF16),
            dma((2, nc)), dma((no,)), dma, dma((mp - 1,)), dma((mp - 1,)),
            dma((nh,)), dma((nh,)), dma((nh, dp - 1)), dma((nh, dp - 1)),
            dma((nh, dp - 1)), dma((nh, dp - 1)), dma((nh, dp)), dma((nh, dp)),
            dma((no, mp - 1)), dma((no, mp - 1)),
        ],
        compiler_params=pltpu.CompilerParams(
            collective_id=0, has_side_effects=True, vmem_limit_bytes=63 << 20),
    )(tokens, w_gate, w_up, w_down)


def by_collectives(tokens, w_gate, w_up, w_down):
    columns = w_gate.shape[1]
    paired_weights = jnp.concatenate([w_gate, w_up], axis=1)
    partial_terms = jnp.dot(
        lax.all_gather(tokens, "mp", axis=0, tiled=True), paired_weights, preferred_element_type=F32)
    summed = lax.psum_scatter(partial_terms, ("dp", "guide"), scatter_dimension=0, tiled=True)
    hidden_share = (jax.nn.silu(summed[:, :columns]) * summed[:, columns:]).astype(BF16)
    hidden = lax.all_gather(hidden_share, ("dp", "guide"), axis=0, tiled=True)
    output_share = lax.psum_scatter(
        jnp.dot(hidden, w_down, preferred_element_type=F32), "mp", scatter_dimension=0, tiled=True)
    return output_share.astype(BF16)


def solution(mesh):
    mp, dp = mesh.shape["mp"], mesh.shape["dp"]

    def per_device(tokens, w_gate, w_up, w_down):
        whole_chunks = w_gate.shape[1] % (2 * WIDTH) == 0 and w_down.shape[1] % OUT_WIDTH == 0
        if whole_chunks and tokens.shape[0] % 8 == 0 and tokens.shape[0] * mp % (16 * dp) == 0:
            return fused(mp, dp, tokens, w_gate, w_up, w_down)
        return by_collectives(tokens, w_gate, w_up, w_down)

    placed = (
        P(("groups", "mp"), ("dp", "guide")),
        P(("dp", "guide"), "mp"),
        P(("dp", "guide"), "mp"),
        P("mp", ("dp", "guide")),
    )
    return jax.shard_map(
        per_device, mesh=mesh, in_specs=placed,
        out_specs=P(("groups", "mp"), ("dp", "guide")), check_vma=False)
```

```python
import functools

import jax
import jax.numpy as jnp
from jax import lax
from jax.experimental import pallas as pl
from jax.experimental.pallas import tpu as pltpu
from jax.sharding import PartitionSpec as P

MESH = pl.DeviceIdType.MESH
F32, BF16 = jnp.float32, jnp.bfloat16
WIDTH = 256
OUT_WIDTH = 512


def kernel(mp, dp, tokens, w_gate, w_up, w_down, out, *scratch):
    (gate_v, up_v, down_v, tok_in, tok_f, tok, sum1_out, sum1_in, kept, sum2_out, sum2_in,
     hid, part, out_send, out_recv,
     w_sem, down_sem, tok_own, tok_s, tok_r, s1_s, s1_r, s2_s, s2_r, hx_s, hx_r, hp_s, hp_r, c_s, c_r) = scratch
    m, d, g = lax.axis_index("mp"), lax.axis_index("dp"), lax.axis_index("guide")
    rows, depth = tokens.shape
    n_half = gate_v.shape[0] // 2
    n_out = down_v.shape[0]
    share = rows * mp // dp
    other = 1 - g
    far = mp // 2
    ways = ((0, 1), (1, mp - 1))

    def weights(side, c):
        half = other if side == 0 else g
        cols = pl.ds(pl.multiple_of((half * n_half + c) * WIDTH, WIDTH), WIDTH)
        slot = side * n_half + c
        return (pltpu.make_async_copy(w_gate.at[:, cols], gate_v.at[slot], w_sem.at[0, slot]),
                pltpu.make_async_copy(w_up.at[:, cols], up_v.at[slot], w_sem.at[1, slot]))

    def downs(n):
        return pltpu.make_async_copy(
            w_down.at[:, pl.ds(pl.multiple_of(n * OUT_WIDTH, OUT_WIDTH), OUT_WIDTH)], down_v.at[n], down_sem.at[n])

    def halves(way, wide):
        return pl.ds(way * (wide // 2), wide // 2)

    own = pltpu.make_async_copy(tokens, tok_in.at[m], tok_own)
    own.start()
    for side in range(2):
        for copy in weights(side, 0):
            copy.start()

    barrier = pltpu.get_barrier_semaphore()
    for _, j in ways:
        pl.semaphore_signal(barrier, inc=1, device_id={"mp": lax.rem(m + j, mp)}, device_id_type=MESH)
    for j in range(1, dp):
        pl.semaphore_signal(barrier, inc=1, device_id={"dp": lax.rem(d + j, dp)}, device_id_type=MESH)
    pl.semaphore_signal(barrier, inc=1, device_id={"guide": other}, device_id_type=MESH)
    pl.semaphore_wait(barrier, 2 + dp)

    def tok_copy(way, s):
        j = ways[way][1]
        block = tok_in.at[lax.rem(m + (s - 1) * (mp - j), mp)]
        if s == far:
            block = block.at[:, halves(way, depth)]
        return pltpu.make_async_remote_copy(
            src_ref=block, dst_ref=block, send_sem=tok_s.at[way, s - 1], recv_sem=tok_r.at[way, s - 1],
            device_id={"mp": lax.rem(m + j, mp)}, device_id_type=MESH)

    def widen(q):
        tok_f[pl.ds(pl.multiple_of(q * rows, 8), rows), :] = tok_in[q].astype(F32)

    own.wait()
    for way, _ in ways:
        tok_copy(way, 1).start()

    @pl.loop(1, n_half)
    def _(c):
        for side in range(2):
            for copy in weights(side, c):
                copy.start()

    @pl.loop(0, n_out)
    def _(n):
        downs(n).start()

    widen(m)
    for s in range(1, far + 1):
        for way, _ in ways:
            tok_copy(way, s).wait_recv()
            if s < far:
                tok_copy(way, s + 1).start()
        if s < far:
            for _, j in ways:
                widen(lax.rem(m + s * (mp - j), mp))
    widen(lax.rem(m + far, mp))
    tok[...] = tok_f[...].astype(BF16)

    def s1_copy(c):
        return pltpu.make_async_remote_copy(
            src_ref=sum1_out.at[c], dst_ref=sum1_in.at[c], send_sem=s1_s.at[c], recv_sem=s1_r.at[c],
            device_id={"guide": other}, device_id_type=MESH)

    def s2_copy(c, j):
        return pltpu.make_async_remote_copy(
            src_ref=sum2_out.at[c, j - 1], dst_ref=sum2_in.at[c, j - 1],
            send_sem=s2_s.at[c, j - 1], recv_sem=s2_r.at[c, j - 1],
            device_id={"dp": lax.rem(d + j, dp)}, device_id_type=MESH)

    def rows_of(b):
        return pl.ds(pl.multiple_of(b * share, 16), share)

    def pair_sum(c):
        s1_copy(c).wait_recv()
        for j in range(1, dp):
            b = rows_of(lax.rem(d + j, dp))
            for k in range(2):
                sum2_out[c, j - 1, k] = (kept[c, k, b, :] + sum1_in[c, k, b, :]).astype(BF16)
            s2_copy(c, j).start()

    @pl.loop(0, n_half)
    def _(c):
        for copy in weights(0, c):
            copy.wait()
        sum1_out[c, 0] = jnp.dot(tok[...], gate_v[c], preferred_element_type=F32)
        sum1_out[c, 1] = jnp.dot(tok[...], up_v[c], preferred_element_type=F32)
        s1_copy(c).start()
        for copy in weights(1, c):
            copy.wait()
        kept[c, 0] = jnp.dot(tok[...], gate_v[n_half + c], preferred_element_type=F32)
        kept[c, 1] = jnp.dot(tok[...], up_v[n_half + c], preferred_element_type=F32)

        @pl.when(c > 0)
        def _():
            pair_sum(c - 1)

    pair_sum(n_half - 1)

    def block(b, half, c):
        return hid.at[rows_of(b), pl.ds(pl.multiple_of((half * n_half + c) * WIDTH, WIDTH), WIDTH)]

    def hx_copy(c, j):
        return pltpu.make_async_remote_copy(
            src_ref=block(d, g, c), dst_ref=block(d, g, c), send_sem=hx_s.at[c, j - 1], recv_sem=hx_r.at[c, j - 1],
            device_id={"dp": lax.rem(d + j, dp)}, device_id_type=MESH)

    def hp_copy(c, j):
        b = block(lax.rem(d + dp - j, dp), g, c)
        return pltpu.make_async_remote_copy(
            src_ref=b, dst_ref=b, send_sem=hp_s.at[c, j], recv_sem=hp_r.at[c, j],
            device_id={"guide": other}, device_id_type=MESH)

    @pl.loop(0, n_half)
    def _(c):
        gate, up = [kept[c, k, rows_of(d), :] + sum1_in[c, k, rows_of(d), :] for k in range(2)]
        for j in range(1, dp):
            s2_copy(c, j).wait_recv()
            gate = gate + sum2_in[c, j - 1, 0].astype(F32)
            up = up + sum2_in[c, j - 1, 1].astype(F32)
        block(d, g, c)[...] = (gate / (1.0 + jnp.exp(-gate)) * up).astype(BF16)
        for j in range(1, dp):
            hx_copy(c, j).start()
        hp_copy(c, 0).start()

    @pl.loop(0, n_half)
    def _(c):
        for j in range(1, dp):
            hx_copy(c, j).wait_recv()
            hp_copy(c, j).start()

    @pl.loop(0, n_half)
    def _(c):
        for j in range(dp):
            hp_copy(c, j).wait_recv()

    def c_copy(n, way, s):
        cols = halves(way, OUT_WIDTH) if s == far else pl.ds(0, OUT_WIDTH)
        return pltpu.make_async_remote_copy(
            src_ref=out_send.at[n, way, s - 1, :, cols], dst_ref=out_recv.at[n, way, s - 1, :, cols],
            send_sem=c_s.at[n, way, s - 1], recv_sem=c_r.at[n, way, s - 1],
            device_id={"mp": lax.rem(m + ways[way][1], mp)}, device_id_type=MESH)

    def mine(n, way, s, cols):
        q = lax.rem(m + s * ways[way][1], mp)
        return part[n, pl.ds(pl.multiple_of(q * rows, 8), rows), cols]

    def pass_on(n):
        for s in range(far - 1, 0, -1):
            for way, _ in ways:
                c_copy(n, way, s + 1).wait_recv()
                for h in range(2):
                    cols = halves(h, OUT_WIDTH)
                    term = mine(n, way, s, cols)
                    if s + 1 < far or h == way:
                        term = term + out_recv[n, way, s, :, cols].astype(F32)
                    out_send[n, way, s - 1, :, cols] = term.astype(BF16)
                c_copy(n, way, s).start()

    @pl.loop(0, n_out)
    def _(n):
        downs(n).wait()
        part[n] = jnp.dot(hid[...], down_v[n], preferred_element_type=F32)
        for way, _ in ways:
            cols = halves(way, OUT_WIDTH)
            out_send[n, way, far - 1, :, cols] = mine(n, way, far, cols).astype(BF16)
            c_copy(n, way, far).start()

        @pl.when(n > 0)
        def _():
            pass_on(n - 1)

    pass_on(n_out - 1)
    for n in range(n_out):
        acc = mine(n, 0, 0, pl.ds(0, OUT_WIDTH))
        for way, _ in ways:
            c_copy(n, way, 1).wait_recv()
            acc = acc + out_recv[n, way, 0].astype(F32)
        out[:, n * OUT_WIDTH:(n + 1) * OUT_WIDTH] = acc.astype(BF16)

    for way, _ in ways:
        for s in range(1, far + 1):
            tok_copy(way, s).wait_send()

    @pl.loop(0, n_half)
    def _(c):
        s1_copy(c).wait_send()
        for j in range(1, dp):
            s2_copy(c, j).wait_send()
            hx_copy(c, j).wait_send()
        for j in range(dp):
            hp_copy(c, j).wait_send()

    @pl.loop(0, n_out)
    def _(n):
        for way, _ in ways:
            for s in range(1, far + 1):
                c_copy(n, way, s).wait_send()


def fused(mp, dp, tokens, w_gate, w_up, w_down):
    rows, depth = tokens.shape
    cols, wide = w_gate.shape[1], w_down.shape[1]
    nc, nh, no = cols // WIDTH, cols // WIDTH // 2, wide // OUT_WIDTH
    full, share, far = rows * mp, rows * mp // dp, mp // 2
    dma = pltpu.SemaphoreType.DMA
    any_, vmem = pl.BlockSpec(memory_space=pl.ANY), pl.BlockSpec(memory_space=pltpu.VMEM)
    return pl.pallas_call(
        functools.partial(kernel, mp, dp),
        out_shape=jax.ShapeDtypeStruct((rows, wide), BF16),
        in_specs=[any_] * 4,
        out_specs=vmem,
        scratch_shapes=[
            pltpu.VMEM((nc, depth, WIDTH), BF16),
            pltpu.VMEM((nc, depth, WIDTH), BF16),
            pltpu.VMEM((no, cols, OUT_WIDTH), BF16),
            pltpu.VMEM((mp, rows, depth), BF16),
            pltpu.VMEM((full, depth), F32),
            pltpu.VMEM((full, depth), BF16),
            pltpu.VMEM((nh, 2, full, WIDTH), F32),
            pltpu.VMEM((nh, 2, full, WIDTH), F32),
            pltpu.VMEM((nh, 2, full, WIDTH), F32),
            pltpu.VMEM((nh, dp - 1, 2, share, WIDTH), BF16),
            pltpu.VMEM((nh, dp - 1, 2, share, WIDTH), BF16),
            pltpu.VMEM((full, cols), BF16),
            pltpu.VMEM((no, full, OUT_WIDTH), F32),
            pltpu.VMEM((no, 2, far, rows, OUT_WIDTH), BF16),
            pltpu.VMEM((no, 2, far, rows, OUT_WIDTH), BF16),
            dma((2, nc)), dma((no,)), dma, dma((2, far)), dma((2, far)),
            dma((nh,)), dma((nh,)), dma((nh, dp - 1)), dma((nh, dp - 1)),
            dma((nh, dp - 1)), dma((nh, dp - 1)), dma((nh, dp)), dma((nh, dp)),
            dma((no, 2, far)), dma((no, 2, far)),
        ],
        compiler_params=pltpu.CompilerParams(
            collective_id=0, has_side_effects=True, vmem_limit_bytes=63 << 20),
    )(tokens, w_gate, w_up, w_down)


def by_collectives(tokens, w_gate, w_up, w_down):
    columns = w_gate.shape[1]
    paired_weights = jnp.concatenate([w_gate, w_up], axis=1)
    partial_terms = jnp.dot(
        lax.all_gather(tokens, "mp", axis=0, tiled=True), paired_weights, preferred_element_type=F32)
    summed = lax.psum_scatter(partial_terms, ("dp", "guide"), scatter_dimension=0, tiled=True)
    hidden_share = (jax.nn.silu(summed[:, :columns]) * summed[:, columns:]).astype(BF16)
    hidden = lax.all_gather(hidden_share, ("dp", "guide"), axis=0, tiled=True)
    output_share = lax.psum_scatter(
        jnp.dot(hidden, w_down, preferred_element_type=F32), "mp", scatter_dimension=0, tiled=True)
    return output_share.astype(BF16)


def solution(mesh):
    mp, dp = mesh.shape["mp"], mesh.shape["dp"]

    def per_device(tokens, w_gate, w_up, w_down):
        whole_chunks = w_gate.shape[1] % (2 * WIDTH) == 0 and w_down.shape[1] % OUT_WIDTH == 0
        if whole_chunks and mp % 2 == 0 and mp > 2 and tokens.shape[0] % 8 == 0 and tokens.shape[0] * mp % (16 * dp) == 0:
            return fused(mp, dp, tokens, w_gate, w_up, w_down)
        return by_collectives(tokens, w_gate, w_up, w_down)

    placed = (
        P(("groups", "mp"), ("dp", "guide")),
        P(("dp", "guide"), "mp"),
        P(("dp", "guide"), "mp"),
        P("mp", ("dp", "guide")),
    )
    return jax.shard_map(
        per_device, mesh=mesh, in_specs=placed,
        out_specs=P(("groups", "mp"), ("dp", "guide")), check_vma=False)
```

```python
import functools

import jax
import jax.numpy as jnp
from jax import lax
from jax.experimental import pallas as pl
from jax.experimental.pallas import tpu as pltpu
from jax.sharding import PartitionSpec as P

MESH = pl.DeviceIdType.MESH
F32, BF16 = jnp.float32, jnp.bfloat16
WIDTH = 256
OUT_WIDTH = 512


def kernel(mp, dp, tokens, w_gate, w_up, w_down, out, *scratch):
    (gate_v, up_v, down_v, tok_in, tok_f, tok, sum1_out, sum1_in, kept, sum2_out, sum2_in,
     hid, part, out_send, out_recv,
     w_sem, down_sem, tok_own, tok_s, tok_r, s1_s, s1_r, s2_s, s2_r, hx_s, hx_r, hp_s, hp_r, c_s, c_r) = scratch
    m, d, g = lax.axis_index("mp"), lax.axis_index("dp"), lax.axis_index("guide")
    rows, depth = tokens.shape
    n_half = gate_v.shape[2] // WIDTH
    n_out = down_v.shape[0]
    share = rows * mp // dp
    other = 1 - g
    piece = depth // 2
    peers = sorted(range(1, mp), key=lambda j: -min(j, mp - j))

    def weights(side, c):
        half = other if side == 0 else g
        cols = pl.ds(pl.multiple_of((half * n_half + c) * WIDTH, WIDTH), WIDTH)
        slot = side * n_half + c
        to = pl.ds(pl.multiple_of(c * WIDTH, WIDTH), WIDTH)
        return (pltpu.make_async_copy(w_gate.at[:, cols], gate_v.at[side, :, to], w_sem.at[0, slot]),
                pltpu.make_async_copy(w_up.at[:, cols], up_v.at[side, :, to], w_sem.at[1, slot]))

    def downs(n):
        return pltpu.make_async_copy(
            w_down.at[:, pl.ds(pl.multiple_of(n * OUT_WIDTH, OUT_WIDTH), OUT_WIDTH)], down_v.at[n], down_sem.at[n])

    own = pltpu.make_async_copy(tokens, tok_in.at[m], tok_own)
    own.start()
    for side in range(2):
        @pl.loop(0, n_half)
        def _(c):
            for copy in weights(side, c):
                copy.start()

    @pl.loop(0, n_out)
    def _(n):
        downs(n).start()

    barrier = pltpu.get_barrier_semaphore()
    for j in range(1, mp):
        pl.semaphore_signal(barrier, inc=1, device_id={"mp": lax.rem(m + j, mp)}, device_id_type=MESH)
    for j in range(1, dp):
        pl.semaphore_signal(barrier, inc=1, device_id={"dp": lax.rem(d + j, dp)}, device_id_type=MESH)
    pl.semaphore_signal(barrier, inc=1, device_id={"guide": other}, device_id_type=MESH)
    pl.semaphore_wait(barrier, mp + dp - 1)

    def tok_copy(p, j):
        cols = pl.ds(p * piece, piece)
        return pltpu.make_async_remote_copy(
            src_ref=tokens.at[:, cols], dst_ref=tok_in.at[m, :, cols],
            send_sem=tok_s.at[p, j - 1], recv_sem=tok_r.at[p, j - 1],
            device_id={"mp": lax.rem(m + j, mp)}, device_id_type=MESH)

    for p in range(2):
        for j in peers:
            tok_copy(p, j).start()
    own.wait()

    def gather(p):
        cols = slice(p * piece, (p + 1) * piece)
        for j in range(1, mp):
            tok_copy(p, j).wait_recv()
        for q in range(mp):
            tok_f[q * rows:(q + 1) * rows, :] = tok_in[q, :, cols].astype(F32)
        tok[:, cols] = tok_f[...].astype(BF16)

    gather(0)
    for side, sums in ((0, sum1_out), (1, kept)):
        @pl.loop(0, n_half)
        def _(c):
            for copy in weights(side, c):
                copy.wait()
        for k, held in ((0, gate_v), (1, up_v)):
            value = jnp.dot(tok[:, :piece], held[side, :piece, :], preferred_element_type=F32)
            for c in range(n_half):
                sums[c, k] = value[:, c * WIDTH:(c + 1) * WIDTH]
    gather(1)

    def s1_copy(c):
        return pltpu.make_async_remote_copy(
            src_ref=sum1_out.at[c], dst_ref=sum1_in.at[c], send_sem=s1_s.at[c], recv_sem=s1_r.at[c],
            device_id={"guide": other}, device_id_type=MESH)

    def s2_copy(c, j):
        return pltpu.make_async_remote_copy(
            src_ref=sum2_out.at[c, j - 1], dst_ref=sum2_in.at[c, j - 1],
            send_sem=s2_s.at[c, j - 1], recv_sem=s2_r.at[c, j - 1],
            device_id={"dp": lax.rem(d + j, dp)}, device_id_type=MESH)

    def rows_of(b):
        return pl.ds(pl.multiple_of(b * share, 16), share)

    def pair_sum(c):
        s1_copy(c).wait_recv()
        for j in range(1, dp):
            b = rows_of(lax.rem(d + j, dp))
            for k in range(2):
                sum2_out[c, j - 1, k] = (kept[c, k, b, :] + sum1_in[c, k, b, :]).astype(BF16)
            s2_copy(c, j).start()

    def finish(side, sums, c):
        for k, held in ((0, gate_v), (1, up_v)):
            sums[c, k] += jnp.dot(
                tok[:, piece:], held[side, piece:, c * WIDTH:(c + 1) * WIDTH], preferred_element_type=F32)

    for c in range(n_half):
        finish(0, sum1_out, c)
        s1_copy(c).start()
        finish(1, kept, c)
        if c > 0:
            pair_sum(c - 1)
    pair_sum(n_half - 1)

    def block(b, half, c):
        return hid.at[rows_of(b), pl.ds(pl.multiple_of((half * n_half + c) * WIDTH, WIDTH), WIDTH)]

    def hx_copy(c, j):
        return pltpu.make_async_remote_copy(
            src_ref=block(d, g, c), dst_ref=block(d, g, c), send_sem=hx_s.at[c, j - 1], recv_sem=hx_r.at[c, j - 1],
            device_id={"dp": lax.rem(d + j, dp)}, device_id_type=MESH)

    def hp_copy(c, j):
        b = block(lax.rem(d + dp - j, dp), g, c)
        return pltpu.make_async_remote_copy(
            src_ref=b, dst_ref=b, send_sem=hp_s.at[c, j], recv_sem=hp_r.at[c, j],
            device_id={"guide": other}, device_id_type=MESH)

    @pl.loop(0, n_half)
    def _(c):
        gate, up = [kept[c, k, rows_of(d), :] + sum1_in[c, k, rows_of(d), :] for k in range(2)]
        for j in range(1, dp):
            s2_copy(c, j).wait_recv()
            gate = gate + sum2_in[c, j - 1, 0].astype(F32)
            up = up + sum2_in[c, j - 1, 1].astype(F32)
        block(d, g, c)[...] = (gate / (1.0 + jnp.exp(-gate)) * up).astype(BF16)
        for j in range(1, dp):
            hx_copy(c, j).start()
        hp_copy(c, 0).start()

    @pl.loop(0, n_half)
    def _(c):
        for j in range(1, dp):
            hx_copy(c, j).wait_recv()
            hp_copy(c, j).start()

    @pl.loop(0, n_half)
    def _(c):
        for j in range(dp):
            hp_copy(c, j).wait_recv()

    def c_copy(n, j):
        return pltpu.make_async_remote_copy(
            src_ref=out_send.at[n, j - 1], dst_ref=out_recv.at[n, j - 1],
            send_sem=c_s.at[n, j - 1], recv_sem=c_r.at[n, j - 1],
            device_id={"mp": lax.rem(m + j, mp)}, device_id_type=MESH)

    def out_rows(q):
        return pl.ds(pl.multiple_of(q * rows, 8), rows)

    for n in range(n_out):
        downs(n).wait()
        part[n] = jnp.dot(hid[...], down_v[n], preferred_element_type=F32)
        for j in peers:
            out_send[n, j - 1] = part[n, out_rows(lax.rem(m + j, mp)), :].astype(BF16)
            c_copy(n, j).start()

    for n in range(n_out):
        acc = part[n, out_rows(m), :]
        for j in range(1, mp):
            c_copy(n, j).wait_recv()
            acc = acc + out_recv[n, j - 1].astype(F32)
        out[:, n * OUT_WIDTH:(n + 1) * OUT_WIDTH] = acc.astype(BF16)

    for p in range(2):
        for j in range(1, mp):
            tok_copy(p, j).wait_send()

    @pl.loop(0, n_half)
    def _(c):
        s1_copy(c).wait_send()
        for j in range(1, dp):
            s2_copy(c, j).wait_send()
            hx_copy(c, j).wait_send()
        for j in range(dp):
            hp_copy(c, j).wait_send()

    @pl.loop(0, n_out)
    def _(n):
        for j in range(1, mp):
            c_copy(n, j).wait_send()


def fused(mp, dp, tokens, w_gate, w_up, w_down):
    rows, depth = tokens.shape
    cols, wide = w_gate.shape[1], w_down.shape[1]
    nc, nh, no = cols // WIDTH, cols // WIDTH // 2, wide // OUT_WIDTH
    full, share = rows * mp, rows * mp // dp
    dma = pltpu.SemaphoreType.DMA
    any_, vmem = pl.BlockSpec(memory_space=pl.ANY), pl.BlockSpec(memory_space=pltpu.VMEM)
    return pl.pallas_call(
        functools.partial(kernel, mp, dp),
        out_shape=jax.ShapeDtypeStruct((rows, wide), BF16),
        in_specs=[any_] * 4,
        out_specs=vmem,
        scratch_shapes=[
            pltpu.VMEM((2, depth, cols // 2), BF16),
            pltpu.VMEM((2, depth, cols // 2), BF16),
            pltpu.VMEM((no, cols, OUT_WIDTH), BF16),
            pltpu.VMEM((mp, rows, depth), BF16),
            pltpu.VMEM((full, depth // 2), F32),
            pltpu.VMEM((full, depth), BF16),
            pltpu.VMEM((nh, 2, full, WIDTH), F32),
            pltpu.VMEM((nh, 2, full, WIDTH), F32),
            pltpu.VMEM((nh, 2, full, WIDTH), F32),
            pltpu.VMEM((nh, dp - 1, 2, share, WIDTH), BF16),
            pltpu.VMEM((nh, dp - 1, 2, share, WIDTH), BF16),
            pltpu.VMEM((full, cols), BF16),
            pltpu.VMEM((no, full, OUT_WIDTH), F32),
            pltpu.VMEM((no, mp - 1, rows, OUT_WIDTH), BF16),
            pltpu.VMEM((no, mp - 1, rows, OUT_WIDTH), BF16),
            dma((2, nc)), dma((no,)), dma, dma((2, mp - 1)), dma((2, mp - 1)),
            dma((nh,)), dma((nh,)), dma((nh, dp - 1)), dma((nh, dp - 1)),
            dma((nh, dp - 1)), dma((nh, dp - 1)), dma((nh, dp)), dma((nh, dp)),
            dma((no, mp - 1)), dma((no, mp - 1)),
        ],
        compiler_params=pltpu.CompilerParams(
            collective_id=0, has_side_effects=True, vmem_limit_bytes=63 << 20),
    )(tokens, w_gate, w_up, w_down)


def by_collectives(tokens, w_gate, w_up, w_down):
    columns = w_gate.shape[1]
    paired_weights = jnp.concatenate([w_gate, w_up], axis=1)
    partial_terms = jnp.dot(
        lax.all_gather(tokens, "mp", axis=0, tiled=True), paired_weights, preferred_element_type=F32)
    summed = lax.psum_scatter(partial_terms, ("dp", "guide"), scatter_dimension=0, tiled=True)
    hidden_share = (jax.nn.silu(summed[:, :columns]) * summed[:, columns:]).astype(BF16)
    hidden = lax.all_gather(hidden_share, ("dp", "guide"), axis=0, tiled=True)
    output_share = lax.psum_scatter(
        jnp.dot(hidden, w_down, preferred_element_type=F32), "mp", scatter_dimension=0, tiled=True)
    return output_share.astype(BF16)


def solution(mesh):
    mp, dp = mesh.shape["mp"], mesh.shape["dp"]

    def per_device(tokens, w_gate, w_up, w_down):
        whole_chunks = w_gate.shape[1] % (2 * WIDTH) == 0 and w_down.shape[1] % OUT_WIDTH == 0
        if whole_chunks and mp > 1 and tokens.shape[1] % 512 == 0 and tokens.shape[0] % 8 == 0 and tokens.shape[0] * mp % (16 * dp) == 0:
            return fused(mp, dp, tokens, w_gate, w_up, w_down)
        return by_collectives(tokens, w_gate, w_up, w_down)

    placed = (
        P(("groups", "mp"), ("dp", "guide")),
        P(("dp", "guide"), "mp"),
        P(("dp", "guide"), "mp"),
        P("mp", ("dp", "guide")),
    )
    return jax.shard_map(
        per_device, mesh=mesh, in_specs=placed,
        out_specs=P(("groups", "mp"), ("dp", "guide")), check_vma=False)
```

```python
import functools

import jax
import jax.numpy as jnp
from jax import lax
from jax.experimental import pallas as pl
from jax.experimental.pallas import tpu as pltpu
from jax.sharding import PartitionSpec as P

MESH = pl.DeviceIdType.MESH
F32, BF16 = jnp.float32, jnp.bfloat16
WIDTH = 256
OUT_WIDTH = 512


def kernel(mp, dp, tokens, w_gate, w_up, w_down, out, *scratch):
    (gate_v, up_v, down_v, tok_in, tok_f, tok, sum1_out, sum1_in, kept, sum2_out, sum2_in,
     hid, part, out_send, out_recv,
     w_sem, down_sem, tok_own, tok_s, tok_r, s1_s, s1_r, s2_s, s2_r, hx_s, hx_r, hp_s, hp_r, c_s, c_r) = scratch
    m, d, g = lax.axis_index("mp"), lax.axis_index("dp"), lax.axis_index("guide")
    rows, depth = tokens.shape
    n_half = gate_v.shape[2] // WIDTH
    n_out = down_v.shape[0]
    share = rows * mp // dp
    other = 1 - g
    piece = depth // 2
    peers = range(mp - 1, 0, -1)

    def weights(side, c):
        half = other if side == 0 else g
        cols = pl.ds(pl.multiple_of((half * n_half + c) * WIDTH, WIDTH), WIDTH)
        slot = side * n_half + c
        to = pl.ds(pl.multiple_of(c * WIDTH, WIDTH), WIDTH)
        return (pltpu.make_async_copy(w_gate.at[:, cols], gate_v.at[side, :, to], w_sem.at[0, slot]),
                pltpu.make_async_copy(w_up.at[:, cols], up_v.at[side, :, to], w_sem.at[1, slot]))

    def downs(n):
        return pltpu.make_async_copy(
            w_down.at[:, pl.ds(pl.multiple_of(n * OUT_WIDTH, OUT_WIDTH), OUT_WIDTH)], down_v.at[n], down_sem.at[n])

    own = pltpu.make_async_copy(tokens, tok_in.at[m], tok_own)
    own.start()
    for side in range(2):
        @pl.loop(0, n_half)
        def _(c):
            for copy in weights(side, c):
                copy.start()

    @pl.loop(0, n_out)
    def _(n):
        downs(n).start()

    barrier = pltpu.get_barrier_semaphore()
    for j in range(1, mp):
        pl.semaphore_signal(barrier, inc=1, device_id={"mp": lax.rem(m + j, mp)}, device_id_type=MESH)
    for j in range(1, dp):
        pl.semaphore_signal(barrier, inc=1, device_id={"dp": lax.rem(d + j, dp)}, device_id_type=MESH)
    pl.semaphore_signal(barrier, inc=1, device_id={"guide": other}, device_id_type=MESH)
    pl.semaphore_wait(barrier, mp + dp - 1)

    def tok_copy(p, j):
        cols = pl.ds(p * piece, piece)
        return pltpu.make_async_remote_copy(
            src_ref=tokens.at[:, cols], dst_ref=tok_in.at[m, :, cols],
            send_sem=tok_s.at[p, j - 1], recv_sem=tok_r.at[p, j - 1],
            device_id={"mp": lax.rem(m + j, mp)}, device_id_type=MESH)

    for p in range(2):
        for j in peers:
            tok_copy(p, j).start()
    own.wait()

    def gather(p):
        cols = slice(p * piece, (p + 1) * piece)
        for j in range(1, mp):
            tok_copy(p, j).wait_recv()
        for q in range(mp):
            tok_f[q * rows:(q + 1) * rows, :] = tok_in[q, :, cols].astype(F32)
        tok[:, cols] = tok_f[...].astype(BF16)

    gather(0)
    for side, sums in ((0, sum1_out), (1, kept)):
        @pl.loop(0, n_half)
        def _(c):
            for copy in weights(side, c):
                copy.wait()
        for k, held in ((0, gate_v), (1, up_v)):
            value = jnp.dot(tok[:, :piece], held[side, :piece, :], preferred_element_type=F32)
            for c in range(n_half):
                sums[c, k] = value[:, c * WIDTH:(c + 1) * WIDTH]
    gather(1)

    def s1_copy(c):
        return pltpu.make_async_remote_copy(
            src_ref=sum1_out.at[c], dst_ref=sum1_in.at[c], send_sem=s1_s.at[c], recv_sem=s1_r.at[c],
            device_id={"guide": other}, device_id_type=MESH)

    def s2_copy(c, j):
        return pltpu.make_async_remote_copy(
            src_ref=sum2_out.at[c, j - 1], dst_ref=sum2_in.at[c, j - 1],
            send_sem=s2_s.at[c, j - 1], recv_sem=s2_r.at[c, j - 1],
            device_id={"dp": lax.rem(d + j, dp)}, device_id_type=MESH)

    def rows_of(b):
        return pl.ds(pl.multiple_of(b * share, 16), share)

    def pair_sum(c):
        s1_copy(c).wait_recv()
        for j in range(1, dp):
            b = rows_of(lax.rem(d + j, dp))
            for k in range(2):
                sum2_out[c, j - 1, k] = (kept[c, k, b, :] + sum1_in[c, k, b, :]).astype(BF16)
            s2_copy(c, j).start()

    def finish(side, sums, c):
        for k, held in ((0, gate_v), (1, up_v)):
            sums[c, k] += jnp.dot(
                tok[:, piece:], held[side, piece:, c * WIDTH:(c + 1) * WIDTH], preferred_element_type=F32)

    for c in range(n_half):
        finish(0, sum1_out, c)
        s1_copy(c).start()
        finish(1, kept, c)
        if c > 0:
            pair_sum(c - 1)
    pair_sum(n_half - 1)

    def block(b, half, c):
        return hid.at[rows_of(b), pl.ds(pl.multiple_of((half * n_half + c) * WIDTH, WIDTH), WIDTH)]

    def hx_copy(c, j):
        return pltpu.make_async_remote_copy(
            src_ref=block(d, g, c), dst_ref=block(d, g, c), send_sem=hx_s.at[c, j - 1], recv_sem=hx_r.at[c, j - 1],
            device_id={"dp": lax.rem(d + j, dp)}, device_id_type=MESH)

    def hp_copy(c, j):
        b = block(lax.rem(d + dp - j, dp), g, c)
        return pltpu.make_async_remote_copy(
            src_ref=b, dst_ref=b, send_sem=hp_s.at[c, j], recv_sem=hp_r.at[c, j],
            device_id={"guide": other}, device_id_type=MESH)

    @pl.loop(0, n_half)
    def _(c):
        gate, up = [kept[c, k, rows_of(d), :] + sum1_in[c, k, rows_of(d), :] for k in range(2)]
        for j in range(1, dp):
            s2_copy(c, j).wait_recv()
            gate = gate + sum2_in[c, j - 1, 0].astype(F32)
            up = up + sum2_in[c, j - 1, 1].astype(F32)
        block(d, g, c)[...] = (gate / (1.0 + jnp.exp(-gate)) * up).astype(BF16)
        for j in range(1, dp):
            hx_copy(c, j).start()
        hp_copy(c, 0).start()

    @pl.loop(0, n_half)
    def _(c):
        for j in range(1, dp):
            hx_copy(c, j).wait_recv()
            hp_copy(c, j).start()

    @pl.loop(0, n_half)
    def _(c):
        for j in range(dp):
            hp_copy(c, j).wait_recv()

    def c_copy(n, j):
        return pltpu.make_async_remote_copy(
            src_ref=out_send.at[n, j - 1], dst_ref=out_recv.at[n, j - 1],
            send_sem=c_s.at[n, j - 1], recv_sem=c_r.at[n, j - 1],
            device_id={"mp": lax.rem(m + j, mp)}, device_id_type=MESH)

    def out_rows(q):
        return pl.ds(pl.multiple_of(q * rows, 8), rows)

    @pl.loop(0, n_out)
    def _(n):
        downs(n).wait()
        part[n] = jnp.dot(hid[...], down_v[n], preferred_element_type=F32)
        for j in peers:
            out_send[n, j - 1] = part[n, out_rows(lax.rem(m + j, mp)), :].astype(BF16)
            c_copy(n, j).start()

    for n in range(n_out):
        acc = part[n, out_rows(m), :]
        for j in range(1, mp):
            c_copy(n, j).wait_recv()
            acc = acc + out_recv[n, j - 1].astype(F32)
        out[:, n * OUT_WIDTH:(n + 1) * OUT_WIDTH] = acc.astype(BF16)

    for p in range(2):
        for j in range(1, mp):
            tok_copy(p, j).wait_send()

    @pl.loop(0, n_half)
    def _(c):
        s1_copy(c).wait_send()
        for j in range(1, dp):
            s2_copy(c, j).wait_send()
            hx_copy(c, j).wait_send()
        for j in range(dp):
            hp_copy(c, j).wait_send()

    @pl.loop(0, n_out)
    def _(n):
        for j in range(1, mp):
            c_copy(n, j).wait_send()


def fused(mp, dp, tokens, w_gate, w_up, w_down):
    rows, depth = tokens.shape
    cols, wide = w_gate.shape[1], w_down.shape[1]
    nc, nh, no = cols // WIDTH, cols // WIDTH // 2, wide // OUT_WIDTH
    full, share = rows * mp, rows * mp // dp
    dma = pltpu.SemaphoreType.DMA
    any_, vmem = pl.BlockSpec(memory_space=pl.ANY), pl.BlockSpec(memory_space=pltpu.VMEM)
    return pl.pallas_call(
        functools.partial(kernel, mp, dp),
        out_shape=jax.ShapeDtypeStruct((rows, wide), BF16),
        in_specs=[any_] * 4,
        out_specs=vmem,
        scratch_shapes=[
            pltpu.VMEM((2, depth, cols // 2), BF16),
            pltpu.VMEM((2, depth, cols // 2), BF16),
            pltpu.VMEM((no, cols, OUT_WIDTH), BF16),
            pltpu.VMEM((mp, rows, depth), BF16),
            pltpu.VMEM((full, depth // 2), F32),
            pltpu.VMEM((full, depth), BF16),
            pltpu.VMEM((nh, 2, full, WIDTH), F32),
            pltpu.VMEM((nh, 2, full, WIDTH), F32),
            pltpu.VMEM((nh, 2, full, WIDTH), F32),
            pltpu.VMEM((nh, dp - 1, 2, share, WIDTH), BF16),
            pltpu.VMEM((nh, dp - 1, 2, share, WIDTH), BF16),
            pltpu.VMEM((full, cols), BF16),
            pltpu.VMEM((no, full, OUT_WIDTH), F32),
            pltpu.VMEM((no, mp - 1, rows, OUT_WIDTH), BF16),
            pltpu.VMEM((no, mp - 1, rows, OUT_WIDTH), BF16),
            dma((2, nc)), dma((no,)), dma, dma((2, mp - 1)), dma((2, mp - 1)),
            dma((nh,)), dma((nh,)), dma((nh, dp - 1)), dma((nh, dp - 1)),
            dma((nh, dp - 1)), dma((nh, dp - 1)), dma((nh, dp)), dma((nh, dp)),
            dma((no, mp - 1)), dma((no, mp - 1)),
        ],
        compiler_params=pltpu.CompilerParams(
            collective_id=0, has_side_effects=True, vmem_limit_bytes=63 << 20),
    )(tokens, w_gate, w_up, w_down)


def by_collectives(tokens, w_gate, w_up, w_down):
    columns = w_gate.shape[1]
    paired_weights = jnp.concatenate([w_gate, w_up], axis=1)
    partial_terms = jnp.dot(
        lax.all_gather(tokens, "mp", axis=0, tiled=True), paired_weights, preferred_element_type=F32)
    summed = lax.psum_scatter(partial_terms, ("dp", "guide"), scatter_dimension=0, tiled=True)
    hidden_share = (jax.nn.silu(summed[:, :columns]) * summed[:, columns:]).astype(BF16)
    hidden = lax.all_gather(hidden_share, ("dp", "guide"), axis=0, tiled=True)
    output_share = lax.psum_scatter(
        jnp.dot(hidden, w_down, preferred_element_type=F32), "mp", scatter_dimension=0, tiled=True)
    return output_share.astype(BF16)


def solution(mesh):
    mp, dp = mesh.shape["mp"], mesh.shape["dp"]

    def per_device(tokens, w_gate, w_up, w_down):
        whole_chunks = w_gate.shape[1] % (2 * WIDTH) == 0 and w_down.shape[1] % OUT_WIDTH == 0
        if whole_chunks and mp > 1 and tokens.shape[1] % 512 == 0 and tokens.shape[0] % 8 == 0 and tokens.shape[0] * mp % (16 * dp) == 0:
            return fused(mp, dp, tokens, w_gate, w_up, w_down)
        return by_collectives(tokens, w_gate, w_up, w_down)

    placed = (
        P(("groups", "mp"), ("dp", "guide")),
        P(("dp", "guide"), "mp"),
        P(("dp", "guide"), "mp"),
        P("mp", ("dp", "guide")),
    )
    return jax.shard_map(
        per_device, mesh=mesh, in_specs=placed,
        out_specs=P(("groups", "mp"), ("dp", "guide")), check_vma=False)
```
